32 devices in a mesh: seq: 8 (over y, x, core), tp: 4 (over z).
Axes of the slice: x: 2, y: 2, z: 4, core: 2. Of those that a mesh axis runs over, the one named last changes fastest.
Arguments:
- inputs: bfloat16 [1024, 4096], P('seq', 'tp'), may hold values from -6 to 6
- target: bfloat16 [1024, 4096], P('seq', 'tp'), may hold values from -6 to 6
- feature_slots: int32 [1024, 8, 8], P(None, 'seq'), may hold values from -1 to 8191, as said below
- w_enc: bfloat16 [65536, 4096], P('seq', 'tp'), may hold values from -0.09375 to 0.09375
- b_enc: float32 [65536], P('seq'), may hold values from -1 to 1
- w_dec: bfloat16 [65536, 4096], P('seq', 'tp'), may hold values from -0.75 to 0.75
- b_dec: float32 [4096], P('tp'), may hold values from -3 to 3
- w_skip: bfloat16 [4096, 4096], P('seq', 'tp'), may hold values from -0.09375 to 0.09375
Outputs:
- reconstruction: bfloat16 [1024, 4096], P('seq', 'tp')
- grad_enc: bfloat16 [65536, 4096], P('seq', 'tp')
- grad_dec: bfloat16 [65536, 4096], P('seq', 'tp')
- grad_benc: float32 [65536], P('seq')
- grad_bdec: float32 [4096], P('tp')
- grad_skip: bfloat16 [4096, 4096], P('seq', 'tp')
The draws below stay inside these ranges and needn't reach their ends.
Inputs may be any that keep to these rules, and one draw needn't show every extreme that they name: feature_slots[t, o, j] is a feature number inside block o of 8192 features, or -1 for an empty slot; each token has exactly 64 live slots naming distinct features, at most 8 in one block, and every token fills all 8 slots of at least one block.
All inputs are finite; a program needn't handle non-finite values.
Results may differ from the reference program's by a relative error of at most 0.0059.
Values may be sent and summed in bfloat16 or wider, within the bound.
No kernel may reach another device: no remote copies, remote signals or barrier semaphores. Data moves between devices by JAX's collectives and lax.ppermute only.
A program may use at most 256 MiB of HBM per device.

```python
import jax
import jax.numpy as jnp
from jax import lax

D = 4096
F = 65536
K = 64
SLOT = 8
TOKENS = 1024
N_SEQ = 8


def draw_feature_slots(key, part):
    key_score, key_base, key_stride = jax.random.split(jax.random.fold_in(key, 11), 3)
    slot_width = N_SEQ * SLOT
    position = jnp.arange(slot_width, dtype=jnp.int32)
    owner_of = position // SLOT
    favored = jnp.arange(TOKENS, dtype=jnp.int32) % N_SEQ
    score = jax.random.randint(key_score, (TOKENS, slot_width), 0, 1024)
    score = jnp.where(owner_of[None, :] == favored[:, None], score + 2048, score)
    keyed = score * slot_width + position[None, :]
    order = jnp.argsort(-keyed, axis=1)
    rank = jnp.argsort(order, axis=1)
    live = (rank < K).reshape(TOKENS, N_SEQ, SLOT)
    block_feats = F // N_SEQ
    base = jax.random.randint(key_base, (TOKENS, N_SEQ, 1), 0, block_feats)
    stride = jax.random.randint(key_stride, (TOKENS, N_SEQ, 1), 1, block_feats // SLOT + 1)
    local = (base + jnp.arange(SLOT, dtype=jnp.int32)[None, None, :] * stride) % block_feats
    return jnp.where(live, local, -1).astype(jnp.int32)


def levels(key, shape, cuts, least, top_value):
    loudness, own = 1.0, jax.random.fold_in(key, 6)
    for dim, parts in cuts:
        steps = jnp.exp(jax.random.uniform(jax.random.fold_in(own, dim), (parts,), jnp.float32, least / len(cuts), top_value / len(cuts)))
        loudness = loudness * jnp.repeat(steps, shape[dim] // parts).reshape([-1 if axis == dim else 1 for axis in range(len(shape))])
    return loudness


def normal_values(key, extent, width, bound, cuts=(), kind=jnp.bfloat16):
    drawn = width * jax.random.normal(key, extent, jnp.float32)
    if cuts:
        drawn = drawn * levels(key, extent, cuts, -0.22, 0.18)
    return jnp.clip(drawn, -bound, bound).astype(kind)


def setup_inputs(seed: int = 0) -> dict:
    keys = jax.random.split(jax.random.key(seed), 9)
    inputs = normal_values(keys[0], (TOKENS, D), 1.0, 6.0, ((0, 8), (1, 4)))
    target = normal_values(keys[1], (TOKENS, D), 1.0, 6.0, ((0, 8), (1, 4)))
    feature_slots = draw_feature_slots(jax.random.fold_in(keys[8], 71), 0)
    w_enc = normal_values(keys[3], (F, D), D ** -0.5, 0.09375, ((0, 8), (1, 4)))
    b_enc = jnp.clip(jax.random.uniform(keys[4], (F,), jnp.float32, -1.0, 1.0) * levels(keys[4], (F,), ((0, 8),), -0.4, 0.0), -1.0, 1.0)
    w_dec = normal_values(keys[5], (F, D), K ** -0.5, 0.75, ((0, 8), (1, 4)))
    b_dec = normal_values(keys[6], (D,), 0.5, 3.0, ((0, 4),), jnp.float32)
    w_skip = normal_values(keys[7], (D, D), D ** -0.5, 0.09375, ((0, 8), (1, 4)))
    return dict(inputs=inputs, target=target, feature_slots=feature_slots, w_enc=w_enc, b_enc=b_enc, w_dec=w_dec, b_dec=b_dec, w_skip=w_skip)


def reference(inputs, target, feature_slots, w_enc, b_enc, w_dec, b_dec, w_skip):
    owners = jnp.arange(N_SEQ, dtype=jnp.int32)[None, :, None] * (F // N_SEQ)
    live_mask = feature_slots >= 0
    global_ids = jnp.where(live_mask, feature_slots + owners, 0).astype(jnp.int32).reshape(TOKENS, N_SEQ * SLOT)
    live_float = live_mask.reshape(TOKENS, N_SEQ * SLOT).astype(jnp.float32)
    block_total = TOKENS // 32
    tok_blocks = inputs.reshape(block_total, 32, D)
    id_blocks = global_ids.reshape(block_total, 32, N_SEQ * SLOT)
    start_carry = jnp.zeros((), jnp.float32)

    def encode(carry, item):
        tok_rows, id_rows = item
        weights = w_enc[id_rows].astype(jnp.float32)
        return carry, jnp.einsum("bd,bsd->bs", tok_rows.astype(jnp.float32), weights)

    pre_sum = lax.scan(encode, start_carry, (tok_blocks, id_blocks))[1].reshape(TOKENS, N_SEQ * SLOT)
    preact = pre_sum + b_enc[global_ids]
    active = (jnp.maximum(preact, 0.0) * live_float).astype(jnp.bfloat16)
    act_blocks = active.reshape(block_total, 32, N_SEQ * SLOT)

    def decode(carry, item):
        act_rows, id_rows = item
        weights = w_dec[id_rows].astype(jnp.float32)
        return carry, jnp.einsum("bs,bsd->bd", act_rows.astype(jnp.float32), weights)

    decoded = lax.scan(decode, start_carry, (act_blocks, id_blocks))[1].reshape(TOKENS, D)
    skip_out = jnp.dot(inputs, w_skip, preferred_element_type=jnp.float32)
    predicted = decoded + skip_out + b_dec
    reconstruction = predicted.astype(jnp.bfloat16)
    residual = (predicted - target.astype(jnp.float32)).astype(jnp.bfloat16)
    res_blocks = residual.reshape(block_total, 32, D)

    def backward(carry, item):
        res_rows, id_rows = item
        weights = w_dec[id_rows].astype(jnp.float32)
        return carry, jnp.einsum("bd,bsd->bs", res_rows.astype(jnp.float32), weights)

    back_sum = lax.scan(backward, start_carry, (res_blocks, id_blocks))[1].reshape(TOKENS, N_SEQ * SLOT)
    slope = back_sum * (preact > 0.0).astype(jnp.float32) * live_float
    grad_benc = jnp.zeros((F,), jnp.float32).at[global_ids.reshape(-1)].add(slope.reshape(-1))
    slope_blocks = slope.astype(jnp.bfloat16).reshape(block_total, 32, N_SEQ * SLOT)

    def accumulate(carry, item):
        enc_total, dec_total = carry
        tok_rows, res_rows, id_rows, slope_rows, act_rows = item
        flat_ids = id_rows.reshape(-1)
        enc_terms = slope_rows.astype(jnp.float32)[:, :, None] * tok_rows.astype(jnp.float32)[:, None, :]
        dec_terms = act_rows.astype(jnp.float32)[:, :, None] * res_rows.astype(jnp.float32)[:, None, :]
        enc_total = enc_total.at[flat_ids].add(enc_terms.reshape(-1, D))
        dec_total = dec_total.at[flat_ids].add(dec_terms.reshape(-1, D))
        return (enc_total, dec_total), start_carry

    zero_grads = jnp.zeros((F, D), jnp.float32)
    totals = lax.scan(accumulate, (zero_grads, zero_grads), (tok_blocks, res_blocks, id_blocks, slope_blocks, act_blocks))[0]
    grad_bdec = jnp.sum(residual.astype(jnp.float32), axis=0)
    grad_skip = jnp.dot(inputs.T, residual, preferred_element_type=jnp.float32).astype(jnp.bfloat16)
    return (reconstruction, totals[0].astype(jnp.bfloat16), totals[1].astype(jnp.bfloat16), grad_benc, grad_bdec, grad_skip)
```

```python
import functools

import jax
import jax.numpy as jnp
from jax import lax
from jax.experimental import pallas as pl
from jax.experimental.pallas import tpu as pltpu
from jax.sharding import PartitionSpec as P

VMEM_BYTES = 60 << 20
F32 = jnp.float32
BF16 = jnp.bfloat16


def pick_kernel(sub, ids_ref, x_ref, w_ref, out_ref):
    step = pl.program_id(0)
    tile = w_ref.shape[0]

    @pl.when(step == 0)
    def _():
        out_ref[...] = jnp.zeros_like(out_ref)

    for s in range(tile // sub):
        dots = lax.dot_general(
            w_ref[s * sub : (s + 1) * sub, :],
            x_ref[...],
            (((1,), (1,)), ((), ())),
            preferred_element_type=F32,
        )
        for block in range(out_ref.shape[1] // 128):
            cols = slice(block * 128, (block + 1) * 128)
            ids = ids_ref[:, cols]
            low = ids & 7
            high = (ids >> 3) - (step * (tile // 8) + s * (sub // 8))
            kept = out_ref[:, cols]
            for g in range(sub // 8):
                found = jnp.take_along_axis(dots[g * 8 : (g + 1) * 8, cols], low, axis=0)
                kept = jnp.where(high == g, found, kept)
            out_ref[:, cols] = kept


def pick(ids, x, w, name):
    features, width = w.shape
    slots, tokens = ids.shape
    tile = min(1024, features)
    return pl.pallas_call(
        functools.partial(pick_kernel, min(256, tile)),
        grid=(features // tile,),
        in_specs=[
            pl.BlockSpec((slots, tokens), lambda i: (0, 0)),
            pl.BlockSpec((tokens, width), lambda i: (0, 0)),
            pl.BlockSpec((tile, width), lambda i: (i, 0)),
        ],
        out_specs=pl.BlockSpec((slots, tokens), lambda i: (0, 0)),
        out_shape=jax.ShapeDtypeStruct((slots, tokens), F32),
        compiler_params=pltpu.CompilerParams(vmem_limit_bytes=VMEM_BYTES),
        cost_estimate=pl.CostEstimate(
            flops=2 * features * width * tokens,
            bytes_accessed=2 * features * width,
            transcendentals=0,
        ),
        name=name,
    )(ids, x, w)


def fill_table(ids_ref, val_ref, table, base, block):
    slots = ids_ref.shape[0]
    cols = slice(block * 128, (block + 1) * 128)
    ids = ids_ref[:, cols]
    iota = lax.broadcasted_iota(jnp.int32, (16, 128), 0).astype(BF16)
    vals = [jnp.broadcast_to(val_ref[j : j + 1, cols], (16, 128)) for j in range(slots)]
    for q in range(table.shape[0] // 256):
        near = jnp.clip(ids - (base + q * 256), -1, 256).astype(BF16)
        away = [jnp.broadcast_to(near[j : j + 1], (16, 128)) - iota for j in range(slots)]
        for g in range(16):
            kept = jnp.zeros((16, 128), BF16)
            for j in range(slots):
                kept = jnp.where(away[j] == 16 * g, vals[j], kept)
            table[q * 256 + g * 16 : q * 256 + (g + 1) * 16, cols] = kept


def grad_kernel(sub, ids_ref, val_ref, y_ref, out_ref, table):
    step = pl.program_id(0)
    tile = out_ref.shape[0]
    for s in range(tile // sub):
        rows = slice(s * sub, (s + 1) * sub)
        for block in range(y_ref.shape[0] // 128):
            fill_table(ids_ref, val_ref, table.at[rows], step * tile + s * sub, block)
        out_ref[rows, :] = jnp.dot(
            table[rows, :], y_ref[...], preferred_element_type=F32
        ).astype(out_ref.dtype)


def grad_rows(ids, val, y, features, name):
    slots, tokens = ids.shape
    width = y.shape[1]
    tile = min(1024, features)
    return pl.pallas_call(
        functools.partial(grad_kernel, min(256, tile)),
        grid=(features // tile,),
        in_specs=[
            pl.BlockSpec((slots, tokens), lambda i: (0, 0)),
            pl.BlockSpec((slots, tokens), lambda i: (0, 0)),
            pl.BlockSpec((tokens, width), lambda i: (0, 0)),
        ],
        out_specs=pl.BlockSpec((tile, width), lambda i: (i, 0)),
        out_shape=jax.ShapeDtypeStruct((features, width), BF16),
        scratch_shapes=[pltpu.VMEM((tile, tokens), BF16)],
        compiler_params=pltpu.CompilerParams(vmem_limit_bytes=VMEM_BYTES),
        cost_estimate=pl.CostEstimate(
            flops=2 * features * width * tokens,
            bytes_accessed=2 * features * width,
            transcendentals=0,
        ),
        name=name,
    )(ids, val, y)


def decode_kernel(sub, ids_ref, val_ref, w_ref, out_ref, table):
    step = pl.program_id(0)
    tile = w_ref.shape[0]

    @pl.when(step == 0)
    def _():
        out_ref[...] = jnp.zeros_like(out_ref)

    for block in range(out_ref.shape[0] // 128):
        for s in range(tile // sub):
            part = table.at[s * sub : (s + 1) * sub]
            fill_table(ids_ref, val_ref, part, step * tile + s * sub, block)
        rows = slice(block * 128, (block + 1) * 128)
        out_ref[rows, :] += lax.dot_general(
            table[:, rows], w_ref[...], (((0,), (0,)), ((), ())), preferred_element_type=F32
        )


def decode(ids, val, w):
    features, width = w.shape
    slots, tokens = ids.shape
    tile = min(1024, features)
    return pl.pallas_call(
        functools.partial(decode_kernel, min(256, tile)),
        grid=(features // tile,),
        in_specs=[
            pl.BlockSpec((slots, tokens), lambda i: (0, 0)),
            pl.BlockSpec((slots, tokens), lambda i: (0, 0)),
            pl.BlockSpec((tile, width), lambda i: (i, 0)),
        ],
        out_specs=pl.BlockSpec((tokens, width), lambda i: (0, 0)),
        out_shape=jax.ShapeDtypeStruct((tokens, width), F32),
        scratch_shapes=[pltpu.VMEM((tile, tokens), BF16)],
        compiler_params=pltpu.CompilerParams(vmem_limit_bytes=VMEM_BYTES),
        cost_estimate=pl.CostEstimate(
            flops=2 * features * width * tokens,
            bytes_accessed=2 * features * width,
            transcendentals=0,
        ),
        name="decode",
    )(ids, val, w)


def bias_kernel(ids_ref, b_ref, out_ref):
    for block in range(out_ref.shape[1] // 128):
        cols = slice(block * 128, (block + 1) * 128)
        ids = ids_ref[:, cols]
        low = ids & 127
        high = ids >> 7
        kept = jnp.zeros(ids.shape, F32)
        for a in range(b_ref.shape[0]):
            row = jnp.broadcast_to(b_ref[a : a + 1, :], ids.shape)
            kept = jnp.where(high == a, jnp.take_along_axis(row, low, axis=1), kept)
        out_ref[:, cols] = kept


def bias_of(ids, bias):
    table = bias.reshape(-1, 128)
    return pl.pallas_call(
        bias_kernel,
        out_shape=jax.ShapeDtypeStruct(ids.shape, F32),
        cost_estimate=pl.CostEstimate(flops=1 << 20, bytes_accessed=1 << 20, transcendentals=0),
        name="bias_of",
    )(ids, table)


def bias_grad_kernel(ids_ref, slope_ref, out_ref):
    slots, tokens = ids_ref.shape
    groups = out_ref.shape[0]
    total = jnp.zeros((groups, 128), F32)
    for j in range(slots):
        ids = ids_ref[j : j + 1, :]
        slope = slope_ref[j : j + 1, :]
        first = slope.astype(BF16).astype(F32)
        second = (slope - first).astype(BF16).astype(F32)
        third = slope - first - second
        high = lax.broadcasted_iota(jnp.int32, (groups, tokens), 0) == (ids >> 7)
        low = lax.broadcasted_iota(jnp.int32, (128, tokens), 0) == (ids & 127)
        low = jnp.where(low, 1.0, 0.0).astype(BF16)
        for part in (first, second, third):
            spread = jnp.where(high, part, 0.0).astype(BF16)
            total = total + lax.dot_general(
                spread, low, (((1,), (1,)), ((), ())), preferred_element_type=F32
            )
    out_ref[...] = total


def bias_grad(ids, slope, features):
    out = pl.pallas_call(
        bias_grad_kernel,
        out_shape=jax.ShapeDtypeStruct((features // 128, 128), F32),
        cost_estimate=pl.CostEstimate(flops=1 << 28, bytes_accessed=1 << 20, transcendentals=0),
        name="bias_grad",
    )(ids, slope)
    return out.reshape(features)


def swap(value, axis, mask):
    size = lax.axis_size(axis)
    return lax.ppermute(value, axis, [(i, i ^ mask) for i in range(size)])


def sum_over(value, axis):
    mask = 1
    while mask < lax.axis_size(axis):
        value = value + swap(value, axis, mask)
        mask *= 2
    return value


def gather_rows(value):
    size = lax.axis_size("seq")
    even = jnp.concatenate([value] + [swap(value, "seq", d) for d in range(2, size, 2)], axis=0)
    return jnp.concatenate([even, swap(even, "seq", 1)], axis=0)


def relative_slots(ids, size):
    slots, tokens = ids.shape
    me = lax.axis_index("seq")
    bits = size.bit_length() - 1
    shaped = ids.reshape((slots,) + (2,) * bits + (tokens // size,))
    for b in range(bits):
        axis = bits - b
        flipped = jnp.flip(shaped, axis)
        shaped = jnp.where((me >> b) & 1 == 1, flipped, shaped)
    shaped = shaped.reshape(slots, size // 2, 2, tokens // size)
    return jnp.swapaxes(shaped, 1, 2).reshape(slots, tokens)


def tree_sum(parts):
    while len(parts) > 1:
        parts = [parts[i] + parts[i + 1] for i in range(0, len(parts), 2)]
    return parts[0]


def skip_columns(inputs, height):
    size, wide = lax.axis_size("seq"), lax.axis_size("tp")
    me, column = lax.axis_index("seq"), lax.axis_index("tp")
    ratio = inputs.shape[1] // height
    pieces = jnp.stack([inputs] + [swap(inputs, "tp", m) for m in range(1, wide)])

    def for_group(mask):
        return lax.dynamic_index_in_dim(pieces, ((me ^ mask) // ratio) ^ column, 0, False)

    even = jnp.concatenate(
        [for_group(0)] + [swap(for_group(d), "seq", d) for d in range(2, size, 2)], axis=0
    )
    mine = lax.dynamic_slice_in_dim(even, (me % 2) * height, height, 1)
    other = lax.dynamic_slice_in_dim(even, (1 - me % 2) * height, height, 1)
    return jnp.concatenate([mine, swap(other, "seq", 1)], axis=0)


def shards(inputs, target, feature_slots, w_enc, b_enc, w_dec, b_dec, w_skip):
    size = lax.axis_size("seq")
    rows = inputs.shape[0]
    half = rows * size // 2
    features = w_enc.shape[0]
    ids = relative_slots(feature_slots[:, 0, :].T, size)
    live = ids >= 0
    all_tokens = gather_rows(inputs)
    skip_inputs = skip_columns(inputs, w_skip.shape[0])

    preact = sum_over(pick(ids, all_tokens, w_enc, "encode"), "tp") + bias_of(ids, b_enc)
    gate = live & (preact > 0.0)
    active = jnp.where(gate, preact, 0.0).astype(BF16)

    terms = decode(ids, active, w_dec)
    terms = terms + jnp.dot(skip_inputs, w_skip, preferred_element_type=F32)
    far = swap(terms[half:].astype(BF16), "seq", 1)
    near = terms[:half] + far.astype(F32)
    sent = near.astype(BF16)
    parts = [near[:rows]] + [
        swap(sent[i * rows : (i + 1) * rows], "seq", 2 * i).astype(F32) for i in range(1, size // 2)
    ]
    predicted = tree_sum(parts) + b_dec
    reconstruction = predicted.astype(BF16)
    residual = (predicted - target.astype(F32)).astype(BF16)

    all_resid = gather_rows(residual)
    slope = sum_over(pick(ids, all_resid, w_dec, "backward"), "tp")
    slope = jnp.where(gate, slope, 0.0)
    grad_dec = grad_rows(ids, active, all_resid, features, "grad_dec")
    grad_enc = grad_rows(ids, slope.astype(BF16), all_tokens, features, "grad_enc")
    grad_benc = bias_grad(ids, slope, features)
    sums = jnp.sum(all_resid.reshape(2, size // 2, rows, -1).astype(F32), axis=2)
    sums = jnp.swapaxes(sums, 0, 1).reshape(size, -1)
    grad_bdec = tree_sum([sums[i] for i in range(size)])
    grad_skip = lax.dot_general(
        skip_inputs, all_resid, (((0,), (0,)), ((), ())), preferred_element_type=F32
    ).astype(BF16)
    return reconstruction, grad_enc, grad_dec, grad_benc, grad_bdec, grad_skip


def solution(mesh):
    in_specs = (
        P("seq", "tp"),
        P("seq", "tp"),
        P(None, "seq", None),
        P("seq", "tp"),
        P("seq"),
        P("seq", "tp"),
        P("tp"),
        P("seq", "tp"),
    )
    out_specs = (P("seq", "tp"), P("seq", "tp"), P("seq", "tp"), P("seq"), P("tp"), P("seq", "tp"))
    return jax.shard_map(shards, mesh=mesh, in_specs=in_specs, out_specs=out_specs, check_vma=False)
```

```python
import functools

import jax
import jax.numpy as jnp
from jax import lax
from jax.experimental import pallas as pl
from jax.experimental.pallas import tpu as pltpu
from jax.sharding import PartitionSpec as P

VMEM_BYTES = 60 << 20
F32 = jnp.float32
BF16 = jnp.bfloat16
GRAD_WIDE = 256
DECODE_WIDE = 256


def whole(i):
    return (0, 0)


def params():
    return pltpu.CompilerParams(vmem_limit_bytes=VMEM_BYTES)


def cost(features, width, tokens):
    return pl.CostEstimate(
        flops=2 * features * width * tokens,
        bytes_accessed=2 * features * width,
        transcendentals=0,
    )


def lay_out(pieces, rows_ref):
    first = 0
    for piece in pieces:
        rows_ref[first : first + piece.shape[0], :] = piece[...]
        first += piece.shape[0]


def tree_sum(parts):
    while len(parts) > 1:
        parts = [parts[i] + parts[i + 1] for i in range(0, len(parts), 2)]
    return parts[0]


def pick_kernel(sub, count, ids_ref, w_ref, *refs):
    pieces, out_ref, rows_ref = refs[:count], refs[count], refs[count + 1]
    step = pl.program_id(0)
    tile = w_ref.shape[0]

    @pl.when(step == 0)
    def _():
        out_ref[...] = jnp.zeros_like(out_ref)
        lay_out(pieces, rows_ref)

    for s in range(tile // sub):
        dots = lax.dot_general(
            w_ref[s * sub : (s + 1) * sub, :],
            rows_ref[...],
            (((1,), (1,)), ((), ())),
            preferred_element_type=F32,
        )
        for block in range(out_ref.shape[1] // 128):
            cols = slice(block * 128, (block + 1) * 128)
            ids = ids_ref[:, cols]
            low = ids & 7
            high = (ids >> 3) - (step * (tile // 8) + s * (sub // 8))
            kept = out_ref[:, cols]
            for g in range(sub // 8):
                found = jnp.take_along_axis(dots[g * 8 : (g + 1) * 8, cols], low, axis=0)
                kept = jnp.where(high == g, found, kept)
            out_ref[:, cols] = kept


def pick(ids, pieces, w, name):
    features, width = w.shape
    slots, tokens = ids.shape
    tile = min(1024, features)
    return pl.pallas_call(
        functools.partial(pick_kernel, min(256, tile), len(pieces)),
        grid=(features // tile,),
        in_specs=[
            pl.BlockSpec((slots, tokens), whole),
            pl.BlockSpec((tile, width), lambda i: (i, 0)),
        ]
        + [pl.BlockSpec(piece.shape, whole) for piece in pieces],
        out_specs=pl.BlockSpec((slots, tokens), whole),
        out_shape=jax.ShapeDtypeStruct((slots, tokens), F32),
        scratch_shapes=[pltpu.VMEM((tokens, width), BF16)],
        compiler_params=params(),
        cost_estimate=cost(features, width, tokens),
        name=name,
    )(ids, w, *pieces)


def slots_at(ids_ref, val_ref, block):
    slots = ids_ref.shape[0]
    cols = slice(block * 128, (block + 1) * 128)
    vals = [jnp.broadcast_to(val_ref[j : j + 1, cols], (16, 128)) for j in range(slots)]
    return ids_ref[:, cols], vals


def table_part(ids, vals, base):
    slots = len(vals)
    iota = lax.broadcasted_iota(jnp.int32, (16, 128), 0).astype(BF16)
    near = jnp.clip(ids - base, -1, 256).astype(BF16)
    away = [jnp.broadcast_to(near[j : j + 1], (16, 128)) - iota for j in range(slots)]
    part = []
    for g in range(16):
        kept = jnp.zeros((16, 128), BF16)
        for j in range(slots):
            kept = jnp.where(away[j] == 16 * g, vals[j], kept)
        part.append(kept)
    return part


def grad_kernel(sub, wide, count, ids_ref, val_ref, *refs):
    pieces, out_ref, rows_ref, tables = refs[:count], refs[count], refs[count + 1], refs[count + 2 :]
    step = pl.program_id(0)
    tile, width = out_ref.shape
    blocks = ids_ref.shape[1] // 128
    subs = tile // sub
    chunks = width // wide

    def build(table, number, some):
        for block in some:
            cols = slice(block * 128, (block + 1) * 128)
            ids, vals = slots_at(ids_ref, val_ref, block)
            for q in range(sub // 256):
                part = table_part(ids, vals, number * sub + q * 256)
                for g in range(16):
                    first = q * 256 + g * 16
                    table[first : first + 16, cols] = part[g]

    @pl.when(step == 0)
    def _():
        lay_out(pieces, rows_ref)
        build(tables[0], 0, range(blocks))

    for s in range(subs):
        here, after = tables[s % 2], tables[(s + 1) % 2]
        for n in range(chunks):
            cols = slice(n * wide, (n + 1) * wide)
            out_ref[s * sub : (s + 1) * sub, cols] = jnp.dot(
                here[...], rows_ref[:, cols], preferred_element_type=F32
            ).astype(out_ref.dtype)
            some = range(n * blocks // chunks, (n + 1) * blocks // chunks)
            build(after, step * subs + s + 1, some)


def grad_rows(ids, val, pieces, features, name):
    slots, tokens = ids.shape
    width = pieces[0].shape[1]
    tile, sub = min(1024, features), 256
    assert (tile // sub) % 2 == 0
    return pl.pallas_call(
        functools.partial(grad_kernel, sub, min(GRAD_WIDE, width), len(pieces)),
        grid=(features // tile,),
        in_specs=[pl.BlockSpec((slots, tokens), whole)] * 2
        + [pl.BlockSpec(piece.shape, whole) for piece in pieces],
        out_specs=pl.BlockSpec((tile, width), lambda i: (i, 0)),
        out_shape=jax.ShapeDtypeStruct((features, width), BF16),
        scratch_shapes=[pltpu.VMEM((tokens, width), BF16)]
        + [pltpu.VMEM((sub, tokens), BF16)] * 2,
        compiler_params=params(),
        cost_estimate=cost(features, width, tokens),
        name=name,
    )(ids, val, *pieces)


def decode_kernel(sub, wide, ids_ref, val_ref, w_ref, keep_ref, send_ref, total, *tables):
    step = pl.program_id(0)
    tile, width = w_ref.shape
    tokens = ids_ref.shape[1]
    subs = tokens // sub
    chunks = width // wide
    work = [(b, q) for b in range(sub // 128) for q in range(tile // 256)]

    def build(table, number, base, n):
        for b, q in work[n * len(work) // chunks : (n + 1) * len(work) // chunks]:
            ids, vals = slots_at(ids_ref, val_ref, number * (sub // 128) + b)
            part = table_part(ids, vals, base + q * 256)
            table[b * 128 : (b + 1) * 128, q * 256 : (q + 1) * 256] = jnp.concatenate(
                part, axis=0
            ).T

    @pl.when(step == 0)
    def _():
        total[...] = jnp.zeros_like(total)
        for n in range(chunks):
            build(tables[0], 0, 0, n)

    for s in range(subs):
        following = (s + 1) % subs
        here, after = tables[s % len(tables)], tables[following % len(tables)]
        base = (step + (s + 1) // subs) * tile
        rows = slice(s * sub, (s + 1) * sub)
        for n in range(chunks):
            cols = slice(n * wide, (n + 1) * wide)
            total[rows, cols] += jnp.dot(here[...], w_ref[:, cols], preferred_element_type=F32)
            build(after, following, base, n)

    @pl.when(step == pl.num_programs(0) - 1)
    def _():
        half = tokens // 2
        keep_ref[...] = total[:half, :]
        send_ref[...] = total[half:, :].astype(BF16)


def decode(ids, val, w, name):
    features, width = w.shape
    slots, tokens = ids.shape
    tile = min(1024, features)
    sub = min(256, tokens // 2)
    subs = tokens // sub
    half = (tokens // 2, width)
    return pl.pallas_call(
        functools.partial(decode_kernel, sub, min(DECODE_WIDE, width)),
        grid=(features // tile,),
        in_specs=[pl.BlockSpec((slots, tokens), whole)] * 2
        + [pl.BlockSpec((tile, width), lambda i: (i, 0))],
        out_specs=[pl.BlockSpec(half, whole)] * 2,
        out_shape=[jax.ShapeDtypeStruct(half, F32), jax.ShapeDtypeStruct(half, BF16)],
        scratch_shapes=[pltpu.VMEM((tokens, width), F32)]
        + [pltpu.VMEM((sub, tile), BF16)] * (2 if subs % 2 == 0 else subs),
        compiler_params=params(),
        cost_estimate=cost(features, width, tokens),
        name=name,
    )(ids, val, w)


def bias_kernel(ids_ref, b_ref, out_ref):
    for block in range(out_ref.shape[1] // 128):
        cols = slice(block * 128, (block + 1) * 128)
        ids = ids_ref[:, cols]
        low = ids & 127
        high = ids >> 7
        kept = jnp.zeros(ids.shape, F32)
        for a in range(b_ref.shape[0]):
            row = jnp.broadcast_to(b_ref[a : a + 1, :], ids.shape)
            kept = jnp.where(high == a, jnp.take_along_axis(row, low, axis=1), kept)
        out_ref[:, cols] = kept


def bias_of(ids, bias):
    table = bias.reshape(-1, 128)
    return pl.pallas_call(
        bias_kernel,
        out_shape=jax.ShapeDtypeStruct(ids.shape, F32),
        cost_estimate=pl.CostEstimate(flops=1 << 20, bytes_accessed=1 << 20, transcendentals=0),
        name="bias_of",
    )(ids, table)


def bias_grad_kernel(ids_ref, slope_ref, out_ref):
    slots, tokens = ids_ref.shape
    groups = out_ref.shape[0]
    total = jnp.zeros((3 * groups, 128), F32)
    for j in range(slots):
        ids = ids_ref[j : j + 1, :]
        slope = slope_ref[j : j + 1, :]
        first = slope.astype(BF16).astype(F32)
        second = (slope - first).astype(BF16).astype(F32)
        third = slope - first - second
        high = lax.broadcasted_iota(jnp.int32, (groups, tokens), 0) == (ids >> 7)
        low = lax.broadcasted_iota(jnp.int32, (128, tokens), 0) == (ids & 127)
        low = jnp.where(low, 1.0, 0.0).astype(BF16)
        spread = jnp.concatenate(
            [jnp.where(high, part, 0.0) for part in (first, second, third)], axis=0
        ).astype(BF16)
        total = total + lax.dot_general(
            spread, low, (((1,), (1,)), ((), ())), preferred_element_type=F32
        )
    out_ref[...] = total[:groups] + total[groups : 2 * groups] + total[2 * groups :]


def bias_grad(ids, slope, features):
    out = pl.pallas_call(
        bias_grad_kernel,
        out_shape=jax.ShapeDtypeStruct((features // 128, 128), F32),
        cost_estimate=pl.CostEstimate(flops=1 << 28, bytes_accessed=1 << 20, transcendentals=0),
        name="bias_grad",
    )(ids, slope)
    return out.reshape(features)


def skip_grad_kernel(count, *refs):
    columns, resid = refs[:count], refs[count : 2 * count]
    out_ref, sum_ref, left, right = refs[2 * count :]
    lay_out(columns, left)
    lay_out(resid, right)
    out_ref[...] = lax.dot_general(
        left[...], right[...], (((0,), (0,)), ((), ())), preferred_element_type=F32
    ).astype(BF16)
    sums = [jnp.sum(piece[...].astype(F32), axis=0, keepdims=True) for piece in resid]
    order = piece_order(count)
    sum_ref[...] = tree_sum([sums[order.index(d)] for d in range(count)])


def skip_grad(columns, resid):
    rows, width = resid[0].shape
    height = columns[0].shape[1]
    count = len(resid)
    out, sums = pl.pallas_call(
        functools.partial(skip_grad_kernel, count),
        out_shape=[
            jax.ShapeDtypeStruct((height, width), BF16),
            jax.ShapeDtypeStruct((1, width), F32),
        ],
        scratch_shapes=[
            pltpu.VMEM((count * rows, height), BF16),
            pltpu.VMEM((count * rows, width), BF16),
        ],
        compiler_params=params(),
        cost_estimate=cost(height, width, count * rows),
        name="skip_grad",
    )(*columns, *resid)
    return out, sums.reshape(width)


def swap(value, axis, mask):
    size = lax.axis_size(axis)
    return lax.ppermute(value, axis, [(i, i ^ mask) for i in range(size)])


def sum_over(value, axis):
    mask = 1
    while mask < lax.axis_size(axis):
        value = value + swap(value, axis, mask)
        mask *= 2
    return value


def piece_order(size):
    return [0, 1] + list(range(2, size, 2)) + list(range(3, size, 2))


def exchange(value):
    size = lax.axis_size("seq")
    near = [value, swap(value, "seq", 1)]
    even = [swap(value, "seq", d) for d in range(2, size, 2)]
    return near, even + [swap(piece, "seq", 1) for piece in even]


def relative_slots(ids, size):
    slots, tokens = ids.shape
    me = lax.axis_index("seq")
    bits = size.bit_length() - 1
    shaped = ids.reshape((slots,) + (2,) * bits + (tokens // size,))
    for b in range(bits):
        axis = bits - b
        flipped = jnp.flip(shaped, axis)
        shaped = jnp.where((me >> b) & 1 == 1, flipped, shaped)
    shaped = shaped.reshape(slots, size, tokens // size)
    return jnp.concatenate([shaped[:, d] for d in piece_order(size)], axis=1)


def skip_groups(inputs, height, after):
    size, wide = lax.axis_size("seq"), lax.axis_size("tp")
    me, column = lax.axis_index("seq"), lax.axis_index("tp")
    assert 2 * height == inputs.shape[1]
    pieces = jnp.stack([inputs] + [swap(inputs, "tp", m) for m in range(1, wide)])
    pieces, after = lax.optimization_barrier((pieces, after))

    def for_group(mask):
        return lax.dynamic_index_in_dim(pieces, ((me ^ mask) // 2) ^ column, 0, False)

    groups = [for_group(0)] + [swap(for_group(d), "seq", d) for d in range(2, size, 2)]
    return groups, after


def shards(inputs, target, feature_slots, w_enc, b_enc, w_dec, b_dec, w_skip):
    size = lax.axis_size("seq")
    me = lax.axis_index("seq")
    rows = inputs.shape[0]
    features = w_enc.shape[0]
    height = w_skip.shape[0]
    ids = relative_slots(feature_slots[:, 0, :].T, size)
    near_ids, far_ids = ids[:, : 2 * rows], ids[:, 2 * rows :]
    live = ids >= 0

    other_skip = swap(w_skip, "seq", 1)
    near_tokens, far_tokens = exchange(inputs)
    near_pre = pick(near_ids, near_tokens, w_enc, "encode_near")
    far_pre = pick(far_ids, far_tokens, w_enc, "encode_far")
    groups, far_pre = skip_groups(inputs, height, far_pre)
    preact = sum_over(jnp.concatenate([near_pre, far_pre], axis=1), "tp") + bias_of(ids, b_enc)
    gate = live & (preact > 0.0)
    active = jnp.where(gate, preact, 0.0).astype(BF16)

    far_keep, far_send = decode(far_ids, active[:, 2 * rows :], w_dec, "decode_far")
    group = jnp.concatenate(groups, axis=0)
    mine = lax.dynamic_slice_in_dim(group, (me % 2) * height, height, 1)
    other = lax.dynamic_slice_in_dim(group, (1 - me % 2) * height, height, 1)
    skip = jnp.dot(mine, w_skip, preferred_element_type=F32) + jnp.dot(
        other, other_skip, preferred_element_type=F32
    )
    sent = (far_keep + swap(far_send, "seq", 1).astype(F32) + skip[rows:]).astype(BF16)
    near_active, sent = lax.optimization_barrier((active[:, : 2 * rows], sent))
    near_keep, near_send = decode(near_ids, near_active, w_dec, "decode_near")
    parts = [near_keep + swap(near_send, "seq", 1).astype(F32) + skip[:rows]] + [
        swap(sent[i * rows : (i + 1) * rows], "seq", 2 * i + 2).astype(F32)
        for i in range(size // 2 - 1)
    ]
    predicted = tree_sum(parts) + b_dec
    reconstruction = predicted.astype(BF16)
    residual = (predicted - target.astype(F32)).astype(BF16)

    near_resid, far_resid = exchange(residual)
    near_slope = pick(near_ids, near_resid, w_dec, "backward_near")
    far_slope = pick(far_ids, far_resid, w_dec, "backward_far")
    slope = sum_over(jnp.concatenate([near_slope, far_slope], axis=1), "tp")
    slope = jnp.where(gate, slope, 0.0)
    resid = near_resid + far_resid
    grad_dec = grad_rows(ids, active, resid, features, "grad_dec")
    grad_enc = grad_rows(ids, slope.astype(BF16), near_tokens + far_tokens, features, "grad_enc")
    grad_benc = bias_grad(ids, slope, features)
    mine = [mine[i * rows : (i + 1) * rows] for i in range(size // 2)]
    others = swap(other, "seq", 1)
    others = [others[i * rows : (i + 1) * rows] for i in range(size // 2)]
    columns = [mine[0], others[0]] + mine[1:] + others[1:]
    grad_skip, grad_bdec = skip_grad(columns, resid)
    return reconstruction, grad_enc, grad_dec, grad_benc, grad_bdec, grad_skip


def solution(mesh):
    in_specs = (
        P("seq", "tp"),
        P("seq", "tp"),
        P(None, "seq", None),
        P("seq", "tp"),
        P("seq"),
        P("seq", "tp"),
        P("tp"),
        P("seq", "tp"),
    )
    out_specs = (P("seq", "tp"), P("seq", "tp"), P("seq", "tp"), P("seq"), P("tp"), P("seq", "tp"))
    return jax.shard_map(shards, mesh=mesh, in_specs=in_specs, out_specs=out_specs, check_vma=False)
```

```python
import functools

import jax
import jax.numpy as jnp
from jax import lax
from jax.experimental import pallas as pl
from jax.experimental.pallas import tpu as pltpu
from jax.sharding import PartitionSpec as P

VMEM_BYTES = 60 << 20
F32 = jnp.float32
BF16 = jnp.bfloat16
GRAD_WIDE = 256
DECODE_WIDE = 256
SPLIT = 2


def whole(i):
    return (0, 0)


def params():
    return pltpu.CompilerParams(vmem_limit_bytes=VMEM_BYTES)


def cost(features, width, tokens):
    return pl.CostEstimate(
        flops=2 * features * width * tokens,
        bytes_accessed=2 * features * width,
        transcendentals=0,
    )


def lay_out(pieces, rows_ref):
    first = 0
    for piece in pieces:
        rows_ref[first : first + piece.shape[0], :] = piece[...]
        first += piece.shape[0]


def tree_sum(parts):
    while len(parts) > 1:
        parts = [parts[i] + parts[i + 1] for i in range(0, len(parts), 2)]
    return parts[0]


def pick_kernel(sub, first, start, count, ids_ref, old_ref, *refs):
    pieces, out_ref, rows_ref = refs[SPLIT : SPLIT + count], refs[-2], refs[-1]
    step = pl.program_id(0)
    share = refs[0].shape[0]
    tile = SPLIT * share

    @pl.when(step == 0)
    def _():
        out_ref[...] = old_ref[...]
        lay_out(pieces, rows_ref)

    for s in range(tile // sub):
        offset = s * sub % share
        dots = lax.dot_general(
            refs[s * sub // share][offset : offset + sub, :],
            rows_ref[...],
            (((1,), (1,)), ((), ())),
            preferred_element_type=F32,
        )
        for block in range(rows_ref.shape[0] // 128):
            cols = slice(first + block * 128, first + (block + 1) * 128)
            ids = ids_ref[:, cols]
            low = ids & 7
            high = (ids >> 3) - ((step + start) * (tile // 8) + s * (sub // 8))
            kept = out_ref[:, cols]
            for g in range(sub // 8):
                found = jnp.take_along_axis(
                    dots[g * 8 : (g + 1) * 8, block * 128 : (block + 1) * 128], low, axis=0
                )
                kept = jnp.where(high == g, found, kept)
            out_ref[:, cols] = kept


def pick(ids, old, pieces, w, first, half):
    features, width = w.shape
    slots, tokens = ids.shape
    here = sum(piece.shape[0] for piece in pieces)
    tile = min(2048 if here <= 256 else 1024, features)
    steps = features // tile
    start = 0
    if half is not None:
        steps, start = steps // 2, half * (steps // 2)
    return pl.pallas_call(
        functools.partial(pick_kernel, min(256, tile), first, start, len(pieces)),
        grid=(steps,),
        in_specs=[pl.BlockSpec((slots, tokens), whole)] * 2
        + [
            pl.BlockSpec((tile // SPLIT, width), lambda i, at=at: ((i + start) * SPLIT + at, 0))
            for at in range(SPLIT)
        ]
        + [pl.BlockSpec(piece.shape, whole) for piece in pieces],
        out_specs=pl.BlockSpec((slots, tokens), whole),
        out_shape=jax.ShapeDtypeStruct((slots, tokens), F32),
        scratch_shapes=[pltpu.VMEM((here, width), BF16)],
        compiler_params=params(),
        cost_estimate=cost(steps * tile, width, here),
    )(ids, old, *[w] * SPLIT, *pieces)


def table_part(ids_ref, val_ref, first, number):
    slots = ids_ref.shape[0]
    cols = slice(first, first + 128)
    iota = lax.broadcasted_iota(jnp.int32, (16, 128), 0).astype(BF16)
    vals = [jnp.broadcast_to(val_ref[j : j + 1, cols], (16, 128)) for j in range(slots)]
    near = jnp.clip(ids_ref[:, cols] - number * 256, -1, 256).astype(BF16)
    away = [jnp.broadcast_to(near[j : j + 1], (16, 128)) - iota for j in range(slots)]
    part = []
    for g in range(16):
        kept = jnp.zeros((16, 128), BF16)
        for j in range(slots):
            kept = jnp.where(away[j] == 16 * g, vals[j], kept)
        part.append(kept)
    return part


def grad_kernel(sub, wide, count, ids_ref, val_ref, *refs):
    pieces, (out_ref, rows_ref), tables = refs[:count], refs[count : count + 2], refs[count + 2 :]
    step = pl.program_id(0)
    tile, width = out_ref.shape
    blocks = ids_ref.shape[1] // 128
    subs = tile // sub
    chunks = width // wide

    def build(table, number, some):
        for block in some:
            cols = slice(block * 128, (block + 1) * 128)
            part = table_part(ids_ref, val_ref, block * 128, number)
            for g in range(sub // 16):
                table[g * 16 : (g + 1) * 16, cols] = part[g]

    @pl.when(step == 0)
    def _():
        lay_out(pieces, rows_ref)
        build(tables[0], 0, range(blocks))

    for s in range(subs):
        here, after = tables[s % 2], tables[(s + 1) % 2]
        for n in range(chunks):
            cols = slice(n * wide, (n + 1) * wide)
            out_ref[s * sub : (s + 1) * sub, cols] = jnp.dot(
                here[...], rows_ref[:, cols], preferred_element_type=F32
            ).astype(out_ref.dtype)
            some = range(n * blocks // chunks, (n + 1) * blocks // chunks)
            build(after, step * subs + s + 1, some)


def grad_rows(ids, val, pieces, features):
    slots, tokens = ids.shape
    width = pieces[0].shape[1]
    tile, sub = min(1024, features), 256
    assert sub == 256 and (tile // sub) % 2 == 0
    return pl.pallas_call(
        functools.partial(grad_kernel, sub, min(GRAD_WIDE, width), len(pieces)),
        grid=(features // tile,),
        in_specs=[pl.BlockSpec((slots, tokens), whole)] * 2
        + [pl.BlockSpec(piece.shape, whole) for piece in pieces],
        out_specs=pl.BlockSpec((tile, width), lambda i: (i, 0)),
        out_shape=jax.ShapeDtypeStruct((features, width), BF16),
        scratch_shapes=[pltpu.VMEM((tokens, width), BF16)]
        + [pltpu.VMEM((sub, tokens), BF16)] * 2,
        compiler_params=params(),
        cost_estimate=cost(features, width, tokens),
    )(ids, val, *pieces)


def decode_kernel(sub, deep, wide, first_token, count, ids_ref, val_ref, w_ref, pair_ref, *refs):
    skips, (keep_ref, send_ref, total) = refs[:count], refs[count : count + 3]
    tables = refs[count + 3 :]
    step = pl.program_id(0)
    tile, width = w_ref.shape
    tokens = total.shape[0]
    chunks = width // wide
    items = [(u, s) for u in range(tile // deep) for s in range(tokens // sub)]
    work = [(b, q) for b in range(sub // 128) for q in range(deep // 256)]

    def build(table, item, first, n):
        for b, q in work[n * len(work) // chunks : (n + 1) * len(work) // chunks]:
            block = item[1] * (sub // 128) + b
            number = first + item[0] * (deep // 256) + q
            part = table_part(ids_ref, val_ref, first_token + block * 128, number)
            table[b * 128 : (b + 1) * 128, q * 256 : (q + 1) * 256] = jnp.concatenate(
                part, axis=0
            ).T

    @pl.when(step == 0)
    def _():
        total[...] = jnp.zeros_like(total)
        for n in range(chunks):
            build(tables[0], items[0], 0, n)

    for p, piece in enumerate(skips):
        rows = slice(p * piece.shape[0], (p + 1) * piece.shape[0])
        total[rows, :] += jnp.dot(piece[...], pair_ref[...], preferred_element_type=F32)

    for i, (u, s) in enumerate(items):
        following = (i + 1) % len(items)
        here, after = tables[i % len(tables)], tables[following % len(tables)]
        first = (step + (i + 1) // len(items)) * (tile // 256)
        rows = slice(s * sub, (s + 1) * sub)
        for n in range(chunks):
            cols = slice(n * wide, (n + 1) * wide)
            total[rows, cols] += jnp.dot(
                here[...], w_ref[u * deep : (u + 1) * deep, cols], preferred_element_type=F32
            )
            build(after, items[following], first, n)

    @pl.when(step == pl.num_programs(0) - 1)
    def _():
        half = tokens // 2
        keep_ref[...] = total[:half, :]
        send_ref[...] = total[half:, :].astype(BF16)


def decode(ids, val, w, skips, pair, first, tokens):
    features, width = w.shape
    slots, every = ids.shape
    tile = min(1024, features)
    steps = features // tile
    part = pair.shape[0] // steps
    assert part % 128 == 0
    sub = min(256, tokens)
    deep = tile if tokens > sub else tile // 2
    count = (tile // deep) * (tokens // sub)
    half = (tokens // 2, width)
    return pl.pallas_call(
        functools.partial(
            decode_kernel, sub, deep, min(DECODE_WIDE, width), first, len(skips)
        ),
        grid=(steps,),
        in_specs=[pl.BlockSpec((slots, every), whole)] * 2
        + [pl.BlockSpec((tile, width), lambda i: (i, 0))]
        + [pl.BlockSpec((part, width), lambda i: (i, 0))]
        + [pl.BlockSpec((skip.shape[0], part), lambda i: (0, i)) for skip in skips],
        out_specs=[pl.BlockSpec(half, whole)] * 2,
        out_shape=[jax.ShapeDtypeStruct(half, F32), jax.ShapeDtypeStruct(half, BF16)],
        scratch_shapes=[pltpu.VMEM((tokens, width), F32)]
        + [pltpu.VMEM((sub, deep), BF16)] * (2 if count % 2 == 0 else count),
        compiler_params=params(),
        cost_estimate=cost(features, width, tokens),
    )(ids, val, w, pair, *skips)


def bias_kernel(ids_ref, b_ref, out_ref):
    for block in range(out_ref.shape[1] // 128):
        cols = slice(block * 128, (block + 1) * 128)
        ids = ids_ref[:, cols]
        low = ids & 127
        high = ids >> 7
        kept = jnp.zeros(ids.shape, F32)
        for a in range(b_ref.shape[0]):
            row = jnp.broadcast_to(b_ref[a : a + 1, :], ids.shape)
            kept = jnp.where(high == a, jnp.take_along_axis(row, low, axis=1), kept)
        out_ref[:, cols] = kept


def bias_of(ids, bias):
    table = bias.reshape(-1, 128)
    return pl.pallas_call(
        bias_kernel,
        out_shape=jax.ShapeDtypeStruct(ids.shape, F32),
        cost_estimate=pl.CostEstimate(flops=1 << 20, bytes_accessed=1 << 20, transcendentals=0),
        name="bias_of",
    )(ids, table)


def bias_grad_kernel(ids_ref, slope_ref, out_ref):
    slots, tokens = ids_ref.shape
    groups = out_ref.shape[0]
    total = jnp.zeros((3 * groups, 128), F32)
    for j in range(slots):
        ids = ids_ref[j : j + 1, :]
        slope = slope_ref[j : j + 1, :]
        first = slope.astype(BF16).astype(F32)
        second = (slope - first).astype(BF16).astype(F32)
        third = slope - first - second
        high = lax.broadcasted_iota(jnp.int32, (groups, tokens), 0) == (ids >> 7)
        low = lax.broadcasted_iota(jnp.int32, (128, tokens), 0) == (ids & 127)
        low = jnp.where(low, 1.0, 0.0).astype(BF16)
        spread = jnp.concatenate(
            [jnp.where(high, part, 0.0) for part in (first, second, third)], axis=0
        ).astype(BF16)
        total = total + lax.dot_general(
            spread, low, (((1,), (1,)), ((), ())), preferred_element_type=F32
        )
    out_ref[...] = total[:groups] + total[groups : 2 * groups] + total[2 * groups :]


def bias_grad(ids, slope, features):
    out = pl.pallas_call(
        bias_grad_kernel,
        out_shape=jax.ShapeDtypeStruct((features // 128, 128), F32),
        cost_estimate=pl.CostEstimate(flops=1 << 28, bytes_accessed=1 << 20, transcendentals=0),
        name="bias_grad",
    )(ids, slope)
    return out.reshape(features)


def skip_grad_kernel(count, *refs):
    columns, resid = refs[:count], refs[count : 2 * count]
    out_ref, sum_ref, left, right = refs[2 * count :]
    lay_out(columns, left)
    lay_out(resid, right)
    out_ref[...] = lax.dot_general(
        left[...], right[...], (((0,), (0,)), ((), ())), preferred_element_type=F32
    ).astype(BF16)
    sums = [jnp.sum(piece[...].astype(F32), axis=0, keepdims=True) for piece in resid]
    order = piece_order(count)
    sum_ref[...] = tree_sum([sums[order.index(d)] for d in range(count)])


def skip_grad(columns, resid):
    rows, width = resid[0].shape
    height = columns[0].shape[1]
    count = len(resid)
    out, sums = pl.pallas_call(
        functools.partial(skip_grad_kernel, count),
        out_shape=[
            jax.ShapeDtypeStruct((height, width), BF16),
            jax.ShapeDtypeStruct((1, width), F32),
        ],
        scratch_shapes=[
            pltpu.VMEM((count * rows, height), BF16),
            pltpu.VMEM((count * rows, width), BF16),
        ],
        compiler_params=params(),
        cost_estimate=cost(height, width, count * rows),
        name="skip_grad",
    )(*columns, *resid)
    return out, sums.reshape(width)


def swap(value, axis, mask):
    size = lax.axis_size(axis)
    return lax.ppermute(value, axis, [(i, i ^ mask) for i in range(size)])


def sum_over(value, axis):
    mask = 1
    while mask < lax.axis_size(axis):
        value = value + swap(value, axis, mask)
        mask *= 2
    return value


def piece_order(size):
    return [0, 1] + list(range(2, size, 2)) + list(range(3, size, 2))


def exchange(value):
    size = lax.axis_size("seq")
    near = [value, swap(value, "seq", 1)]
    even = [swap(value, "seq", d) for d in range(2, size, 2)]
    return near, even, [swap(piece, "seq", 1) for piece in even]


def order_kernel(size, me_ref, ids_ref, out_ref):
    rows = ids_ref.shape[1] // size
    for at, d in enumerate(piece_order(size)):
        first = pl.multiple_of((me_ref[0] ^ d) * rows, 128)
        out_ref[:, at * rows : (at + 1) * rows] = ids_ref[:, pl.ds(first, rows)]


def relative_slots(ids, size):
    me = lax.axis_index("seq").astype(jnp.int32).reshape(1)
    return pl.pallas_call(
        functools.partial(order_kernel, size),
        in_specs=[pl.BlockSpec(memory_space=pltpu.SMEM), pl.BlockSpec(memory_space=pltpu.VMEM)],
        out_shape=jax.ShapeDtypeStruct(ids.shape, jnp.int32),
        name="order",
    )(me, ids)


def work(inputs, target, feature_slots, w_enc, b_enc, w_dec, b_dec, w_skip):
    size, wide = lax.axis_size("seq"), lax.axis_size("tp")
    me, column = lax.axis_index("seq"), lax.axis_index("tp")
    rows = inputs.shape[0]
    pair_rows = 2 * rows
    far_rows = (size - 2) * rows
    features = w_enc.shape[0]
    height = w_skip.shape[0]
    assert 2 * height == inputs.shape[1]
    ids = relative_slots(feature_slots[:, 0, :].T, size)
    none = jnp.zeros(ids.shape, F32)

    near_tokens, even_tokens, odd_tokens = exchange(inputs)
    far_tokens = even_tokens + odd_tokens
    columns = [inputs] + [swap(inputs, "tp", m) for m in range(1, wide)]
    other_skip = swap(w_skip, "seq", 1)

    pre = pick(ids, none, near_tokens, w_enc, 0, None)
    pre = pick(ids, pre, far_tokens, w_enc, pair_rows, 0)
    columns, pre = lax.optimization_barrier((columns, pre))
    columns = jnp.stack(columns)

    def for_group(mask):
        return lax.dynamic_index_in_dim(columns, ((me ^ mask) // 2) ^ column, 0, False)

    groups = [for_group(d) for d in range(0, size, 2)]
    groups, pre = lax.optimization_barrier((groups, pre))
    groups = groups[:1] + [
        swap(group, "seq", 2 * d + 2) for d, group in enumerate(groups[1:])
    ]
    pre = pick(ids, pre, far_tokens, w_enc, pair_rows, 1)
    (w_skip, other_skip), pre = lax.optimization_barrier(((w_skip, other_skip), pre))
    first_core = me % 2 == 0
    pair = jnp.concatenate(
        [jnp.where(first_core, w_skip, other_skip), jnp.where(first_core, other_skip, w_skip)]
    )
    preact = sum_over(pre, "tp") + bias_of(ids, b_enc)
    gate = (ids >= 0) & (preact > 0.0)
    active = jnp.where(gate, preact, 0.0).astype(BF16)

    far_keep, far_send = decode(ids, active, w_dec, groups[1:], pair, pair_rows, far_rows)
    sent = (far_keep + swap(far_send, "seq", 1).astype(F32)).astype(BF16)
    sent = [sent[i * rows : (i + 1) * rows] for i in range(size // 2 - 1)]
    near_active, sent = lax.optimization_barrier((active, sent))
    parts = [swap(piece, "seq", 2 * d + 2).astype(F32) for d, piece in enumerate(sent)]
    near_keep, near_send = decode(ids, near_active, w_dec, groups[:1], pair, 0, pair_rows)
    parts = [near_keep + swap(near_send, "seq", 1).astype(F32)] + parts
    predicted = tree_sum(parts) + b_dec
    reconstruction = predicted.astype(BF16)
    residual = (predicted - target.astype(F32)).astype(BF16)

    near_resid, even_resid, odd_resid = exchange(residual)
    back = pick(ids, none, near_resid, w_dec, 0, None)
    far_resid = even_resid + odd_resid
    back = pick(ids, back, far_resid, w_dec, pair_rows, None)
    slope = jnp.where(gate, sum_over(back, "tp"), 0.0)
    resid = near_resid + far_resid
    grad_dec = grad_rows(ids, active, resid, features)
    grad_enc = grad_rows(ids, slope.astype(BF16), near_tokens + far_tokens, features)
    grad_benc = bias_grad(ids, slope, features)
    groups, _ = lax.optimization_barrier((groups, back))
    mine = [lax.dynamic_slice_in_dim(g, (me % 2) * height, height, 1) for g in groups]
    other = [lax.dynamic_slice_in_dim(g, (1 - me % 2) * height, height, 1) for g in groups]
    others = swap(jnp.concatenate(other), "seq", 1)
    others = [others[i * rows : (i + 1) * rows] for i in range(size // 2)]
    grad_skip, grad_bdec = skip_grad([mine[0], others[0]] + mine[1:] + others[1:], resid)
    return reconstruction, grad_enc, grad_dec, grad_benc, grad_bdec, grad_skip


def solution(mesh):
    in_specs = (
        P("seq", "tp"),
        P("seq", "tp"),
        P(None, "seq", None),
        P("seq", "tp"),
        P("seq"),
        P("seq", "tp"),
        P("tp"),
        P("seq", "tp"),
    )
    out_specs = (P("seq", "tp"), P("seq", "tp"), P("seq", "tp"), P("seq"), P("tp"), P("seq", "tp"))
    return jax.shard_map(work, mesh=mesh, in_specs=in_specs, out_specs=out_specs, check_vma=False)
```

```python
import functools

import jax
import jax.numpy as jnp
from jax import lax
from jax.experimental import pallas as pl
from jax.experimental.pallas import tpu as pltpu
from jax.sharding import PartitionSpec as P

VMEM_BYTES = 60 << 20
F32 = jnp.float32
BF16 = jnp.bfloat16
GRAD_WIDE = 512
DECODE_WIDE = 256
SPLIT = 2


def whole(i):
    return (0, 0)


def params():
    return pltpu.CompilerParams(vmem_limit_bytes=VMEM_BYTES)


def cost(features, width, tokens):
    return pl.CostEstimate(
        flops=2 * features * width * tokens,
        bytes_accessed=2 * features * width,
        transcendentals=0,
    )


def lay_out(pieces, rows_ref):
    first = 0
    for piece in pieces:
        rows_ref[first : first + piece.shape[0], :] = piece[...]
        first += piece.shape[0]


def lay_out_blocks(pieces, rows_ref):
    first = 0
    for piece in pieces:
        for block in range(rows_ref.shape[0]):
            rows_ref[block, first : first + piece.shape[0], :] = piece[
                :, block * 128 : (block + 1) * 128
            ]
        first += piece.shape[0]


def from_blocks(ref, first, last):
    return jnp.concatenate([ref[block] for block in range(first, last)], axis=1)


def tree_sum(parts):
    while len(parts) > 1:
        parts = [parts[i] + parts[i + 1] for i in range(0, len(parts), 2)]
    return parts[0]


def pick_kernel(sub, first, start, count, ids_ref, old_ref, *refs):
    pieces, out_ref, rows_ref = refs[SPLIT : SPLIT + count], refs[-2], refs[-1]
    step = pl.program_id(0)
    share = refs[0].shape[0]
    tile = SPLIT * share

    @pl.when(step == 0)
    def _():
        out_ref[...] = old_ref[...]
        lay_out(pieces, rows_ref)

    for s in range(tile // sub):
        offset = s * sub % share
        dots = lax.dot_general(
            refs[s * sub // share][offset : offset + sub, :],
            rows_ref[...],
            (((1,), (1,)), ((), ())),
            preferred_element_type=F32,
        )
        for block in range(rows_ref.shape[0] // 128):
            cols = slice(first + block * 128, first + (block + 1) * 128)
            ids = ids_ref[:, cols]
            low = ids & 7
            high = (ids >> 3) - ((step + start) * (tile // 8) + s * (sub // 8))
            kept = out_ref[:, cols]
            for g in range(sub // 8):
                found = jnp.take_along_axis(
                    dots[g * 8 : (g + 1) * 8, block * 128 : (block + 1) * 128], low, axis=0
                )
                kept = jnp.where(high == g, found, kept)
            out_ref[:, cols] = kept


def pick(ids, old, pieces, w, first, half):
    features, width = w.shape
    slots, tokens = ids.shape
    here = sum(piece.shape[0] for piece in pieces)
    tile = min(2048 if here <= 256 else 1024, features)
    steps = features // tile
    start = 0
    if half is not None:
        steps, start = steps // 2, half * (steps // 2)
    return pl.pallas_call(
        functools.partial(pick_kernel, min(256, tile), first, start, len(pieces)),
        grid=(steps,),
        in_specs=[pl.BlockSpec((slots, tokens), whole)] * 2
        + [
            pl.BlockSpec((tile // SPLIT, width), lambda i, at=at: ((i + start) * SPLIT + at, 0))
            for at in range(SPLIT)
        ]
        + [pl.BlockSpec(piece.shape, whole) for piece in pieces],
        out_specs=pl.BlockSpec((slots, tokens), whole),
        out_shape=jax.ShapeDtypeStruct((slots, tokens), F32),
        scratch_shapes=[pltpu.VMEM((here, width), BF16)],
        compiler_params=params(),
        cost_estimate=cost(steps * tile, width, here),
    )(ids, old, *[w] * SPLIT, *pieces)


def table_part(ids_ref, val_ref, first, number):
    slots = ids_ref.shape[0]
    cols = slice(first, first + 128)
    iota = lax.broadcasted_iota(jnp.int32, (16, 128), 0).astype(BF16)
    vals = [jnp.broadcast_to(val_ref[j : j + 1, cols], (16, 128)) for j in range(slots)]
    near = jnp.clip(ids_ref[:, cols] - number * 256, -1, 256).astype(BF16)
    away = [jnp.broadcast_to(near[j : j + 1], (16, 128)) - iota for j in range(slots)]
    part = []
    for g in range(16):
        kept = jnp.zeros((16, 128), BF16)
        for j in range(slots):
            kept = jnp.where(away[j] == 16 * g, vals[j], kept)
        part.append(kept)
    return part


def grad_kernel(sub, wide, count, ids_ref, val_ref, *refs):
    pieces, (out_ref, rows_ref), tables = refs[:count], refs[count : count + 2], refs[count + 2 :]
    step = pl.program_id(0)
    tile, width = out_ref.shape
    blocks = ids_ref.shape[1] // 128
    subs = tile // sub
    chunks = width // wide

    def build(table, number, some):
        for block in some:
            for q in range(sub // 256):
                part = table_part(ids_ref, val_ref, block * 128, number * (sub // 256) + q)
                for g in range(16):
                    first = q * 256 + g * 16
                    table[block, first : first + 16, :] = part[g]

    @pl.when(step == 0)
    def _():
        lay_out_blocks(pieces, rows_ref)
        build(tables[0], 0, range(blocks))

    for s in range(subs):
        here, after = tables[s % 2], tables[(s + 1) % 2]
        for n in range(chunks):
            cols = slice(n * wide, (n + 1) * wide)
            out_ref[s * sub : (s + 1) * sub, cols] = jnp.dot(
                from_blocks(here, 0, blocks),
                from_blocks(rows_ref, n * wide // 128, (n + 1) * wide // 128),
                preferred_element_type=F32,
            ).astype(out_ref.dtype)
            some = range(n * blocks // chunks, (n + 1) * blocks // chunks)
            build(after, step * subs + s + 1, some)


def grad_rows(ids, val, pieces, features):
    slots, tokens = ids.shape
    width = pieces[0].shape[1]
    tile, sub = min(1024, features), 512
    assert (tile // sub) % 2 == 0
    return pl.pallas_call(
        functools.partial(grad_kernel, sub, min(GRAD_WIDE, width), len(pieces)),
        grid=(features // tile,),
        in_specs=[pl.BlockSpec((slots, tokens), whole)] * 2
        + [pl.BlockSpec(piece.shape, whole) for piece in pieces],
        out_specs=pl.BlockSpec((tile, width), lambda i: (i, 0)),
        out_shape=jax.ShapeDtypeStruct((features, width), BF16),
        scratch_shapes=[pltpu.VMEM((width // 128, tokens, 128), BF16)]
        + [pltpu.VMEM((tokens // 128, sub, 128), BF16)] * 2,
        compiler_params=params(),
        cost_estimate=cost(features, width, tokens),
    )(ids, val, *pieces)


def decode_kernel(sub, deep, wide, first_token, count, ids_ref, val_ref, w_ref, pair_ref, *refs):
    skips, (keep_ref, send_ref, total) = refs[:count], refs[count : count + 3]
    tables = refs[count + 3 :]
    step = pl.program_id(0)
    tile, width = w_ref.shape
    tokens = total.shape[0]
    chunks = width // wide
    items = [(u, s) for u in range(tile // deep) for s in range(tokens // sub)]
    work = [(b, q) for b in range(sub // 128) for q in range(deep // 256)]

    def build(table, item, first, n):
        for b, q in work[n * len(work) // chunks : (n + 1) * len(work) // chunks]:
            block = item[1] * (sub // 128) + b
            number = first + item[0] * (deep // 256) + q
            part = table_part(ids_ref, val_ref, first_token + block * 128, number)
            for h in range(2):
                table[2 * q + h, b * 128 : (b + 1) * 128, :] = jnp.concatenate(
                    part[8 * h : 8 * h + 8], axis=0
                ).T

    @pl.when(step == 0)
    def _():
        total[...] = jnp.zeros_like(total)
        for n in range(chunks):
            build(tables[0], items[0], 0, n)

    for p, piece in enumerate(skips):
        rows = slice(p * piece.shape[0], (p + 1) * piece.shape[0])
        total[rows, :] += jnp.dot(piece[...], pair_ref[...], preferred_element_type=F32)

    for i, (u, s) in enumerate(items):
        following = (i + 1) % len(items)
        here, after = tables[i % len(tables)], tables[following % len(tables)]
        first = (step + (i + 1) // len(items)) * (tile // 256)
        rows = slice(s * sub, (s + 1) * sub)
        for n in range(chunks):
            cols = slice(n * wide, (n + 1) * wide)
            total[rows, cols] += jnp.dot(
                from_blocks(here, 0, deep // 128),
                w_ref[u * deep : (u + 1) * deep, cols],
                preferred_element_type=F32,
            )
            build(after, items[following], first, n)

    @pl.when(step == pl.num_programs(0) - 1)
    def _():
        half = tokens // 2
        keep_ref[...] = total[:half, :]
        send_ref[...] = total[half:, :].astype(BF16)


def decode(ids, val, w, skips, pair, first, tokens):
    features, width = w.shape
    slots, every = ids.shape
    tile = min(2048 if tokens <= 256 else 1024, features)
    steps = features // tile
    part = pair.shape[0] // steps
    assert part % 128 == 0
    sub = min(256, tokens)
    deep = tile if tokens > sub else tile // 2
    count = (tile // deep) * (tokens // sub)
    half = (tokens // 2, width)
    return pl.pallas_call(
        functools.partial(
            decode_kernel, sub, deep, min(DECODE_WIDE, width), first, len(skips)
        ),
        grid=(steps,),
        in_specs=[pl.BlockSpec((slots, every), whole)] * 2
        + [pl.BlockSpec((tile, width), lambda i: (i, 0))]
        + [pl.BlockSpec((part, width), lambda i: (i, 0))]
        + [pl.BlockSpec((skip.shape[0], part), lambda i: (0, i)) for skip in skips],
        out_specs=[pl.BlockSpec(half, whole)] * 2,
        out_shape=[jax.ShapeDtypeStruct(half, F32), jax.ShapeDtypeStruct(half, BF16)],
        scratch_shapes=[pltpu.VMEM((tokens, width), F32)]
        + [pltpu.VMEM((deep // 128, sub, 128), BF16)] * (2 if count % 2 == 0 else count),
        compiler_params=params(),
        cost_estimate=cost(features, width, tokens),
    )(ids, val, w, pair, *skips)


def bias_kernel(ids_ref, b_ref, out_ref):
    for block in range(out_ref.shape[1] // 128):
        cols = slice(block * 128, (block + 1) * 128)
        ids = ids_ref[:, cols]
        low = ids & 127
        high = ids >> 7
        kept = jnp.zeros(ids.shape, F32)
        for a in range(b_ref.shape[0]):
            row = jnp.broadcast_to(b_ref[a : a + 1, :], ids.shape)
            kept = jnp.where(high == a, jnp.take_along_axis(row, low, axis=1), kept)
        out_ref[:, cols] = kept


def bias_of(ids, bias):
    table = bias.reshape(-1, 128)
    return pl.pallas_call(
        bias_kernel,
        out_shape=jax.ShapeDtypeStruct(ids.shape, F32),
        cost_estimate=pl.CostEstimate(flops=1 << 20, bytes_accessed=1 << 20, transcendentals=0),
        name="bias_of",
    )(ids, table)


def bias_grad_kernel(ids_ref, slope_ref, out_ref):
    slots, tokens = ids_ref.shape
    groups = out_ref.shape[0]
    total = jnp.zeros((3 * groups, 128), F32)
    for j in range(slots):
        ids = ids_ref[j : j + 1, :]
        slope = slope_ref[j : j + 1, :]
        first = slope.astype(BF16).astype(F32)
        second = (slope - first).astype(BF16).astype(F32)
        third = slope - first - second
        high = lax.broadcasted_iota(jnp.int32, (groups, tokens), 0) == (ids >> 7)
        low = lax.broadcasted_iota(jnp.int32, (128, tokens), 0) == (ids & 127)
        low = jnp.where(low, 1.0, 0.0).astype(BF16)
        spread = jnp.concatenate(
            [jnp.where(high, part, 0.0) for part in (first, second, third)], axis=0
        ).astype(BF16)
        total = total + lax.dot_general(
            spread, low, (((1,), (1,)), ((), ())), preferred_element_type=F32
        )
    out_ref[...] = total[:groups] + total[groups : 2 * groups] + total[2 * groups :]


def bias_grad(ids, slope, features):
    out = pl.pallas_call(
        bias_grad_kernel,
        out_shape=jax.ShapeDtypeStruct((features // 128, 128), F32),
        cost_estimate=pl.CostEstimate(flops=1 << 28, bytes_accessed=1 << 20, transcendentals=0),
        name="bias_grad",
    )(ids, slope)
    return out.reshape(features)


def skip_grad_kernel(count, *refs):
    columns, resid = refs[:count], refs[count : 2 * count]
    out_ref, sum_ref, left, right = refs[2 * count :]

    @pl.when(pl.program_id(0) == 0)
    def _():
        lay_out(columns, left)

    lay_out(resid, right)
    out_ref[...] = lax.dot_general(
        left[...], right[...], (((0,), (0,)), ((), ())), preferred_element_type=F32
    ).astype(BF16)
    sums = [jnp.sum(piece[...].astype(F32), axis=0, keepdims=True) for piece in resid]
    order = piece_order(count)
    sum_ref[...] = tree_sum([sums[order.index(d)] for d in range(count)])


def skip_grad(columns, resid):
    rows, width = resid[0].shape
    height = columns[0].shape[1]
    count = len(resid)
    wide = min(512, width)
    out, sums = pl.pallas_call(
        functools.partial(skip_grad_kernel, count),
        grid=(width // wide,),
        in_specs=[pl.BlockSpec((rows, height), whole)] * count
        + [pl.BlockSpec((rows, wide), lambda i: (0, i))] * count,
        out_specs=[
            pl.BlockSpec((height, wide), lambda i: (0, i)),
            pl.BlockSpec((1, wide), lambda i: (0, i)),
        ],
        out_shape=[
            jax.ShapeDtypeStruct((height, width), BF16),
            jax.ShapeDtypeStruct((1, width), F32),
        ],
        scratch_shapes=[
            pltpu.VMEM((count * rows, height), BF16),
            pltpu.VMEM((count * rows, wide), BF16),
        ],
        compiler_params=params(),
        cost_estimate=cost(height, width, count * rows),
        name="skip_grad",
    )(*columns, *resid)
    return out, sums.reshape(width)


def swap(value, axis, mask):
    size = lax.axis_size(axis)
    return lax.ppermute(value, axis, [(i, i ^ mask) for i in range(size)])


def sum_over(value, axis):
    mask = 1
    while mask < lax.axis_size(axis):
        value = value + swap(value, axis, mask)
        mask *= 2
    return value


def piece_order(size):
    return [0, 1] + list(range(2, size, 2)) + list(range(3, size, 2))


def exchange(value):
    size = lax.axis_size("seq")
    near = [value, swap(value, "seq", 1)]
    even = [swap(value, "seq", d) for d in range(2, size, 2)]
    return near, even, [swap(piece, "seq", 1) for piece in even]


def order_kernel(size, me_ref, ids_ref, out_ref):
    rows = ids_ref.shape[1] // size
    for at, d in enumerate(piece_order(size)):
        first = pl.multiple_of((me_ref[0] ^ d) * rows, 128)
        out_ref[:, at * rows : (at + 1) * rows] = ids_ref[:, pl.ds(first, rows)]


def relative_slots(ids, size):
    me = lax.axis_index("seq").astype(jnp.int32).reshape(1)
    return pl.pallas_call(
        functools.partial(order_kernel, size),
        in_specs=[pl.BlockSpec(memory_space=pltpu.SMEM), pl.BlockSpec(memory_space=pltpu.VMEM)],
        out_shape=jax.ShapeDtypeStruct(ids.shape, jnp.int32),
        name="order",
    )(me, ids)


def work(inputs, target, feature_slots, w_enc, b_enc, w_dec, b_dec, w_skip):
    size, wide = lax.axis_size("seq"), lax.axis_size("tp")
    me, column = lax.axis_index("seq"), lax.axis_index("tp")
    rows = inputs.shape[0]
    pair_rows = 2 * rows
    far_rows = (size - 2) * rows
    features = w_enc.shape[0]
    height = w_skip.shape[0]
    assert 2 * height == inputs.shape[1]
    ids = relative_slots(feature_slots[:, 0, :].T, size)
    none = jnp.zeros(ids.shape, F32)

    near_tokens, even_tokens, odd_tokens = exchange(inputs)
    far_tokens = even_tokens + odd_tokens
    columns = [inputs] + [swap(inputs, "tp", m) for m in range(1, wide)]
    other_skip = swap(w_skip, "seq", 1)

    pre = pick(ids, none, near_tokens, w_enc, 0, None)
    pre = pick(ids, pre, far_tokens, w_enc, pair_rows, 0)
    columns, pre = lax.optimization_barrier((columns, pre))
    columns = jnp.stack(columns)

    def for_group(mask):
        return lax.dynamic_index_in_dim(columns, ((me ^ mask) // 2) ^ column, 0, False)

    groups = [for_group(d) for d in range(0, size, 2)]
    groups, pre = lax.optimization_barrier((groups, pre))
    groups = groups[:1] + [
        swap(group, "seq", 2 * d + 2) for d, group in enumerate(groups[1:])
    ]
    pre = pick(ids, pre, far_tokens, w_enc, pair_rows, 1)
    (w_skip, other_skip), pre = lax.optimization_barrier(((w_skip, other_skip), pre))
    first_core = me % 2 == 0
    pair = jnp.concatenate(
        [jnp.where(first_core, w_skip, other_skip), jnp.where(first_core, other_skip, w_skip)]
    )
    preact = sum_over(pre, "tp") + bias_of(ids, b_enc)
    gate = (ids >= 0) & (preact > 0.0)
    active = jnp.where(gate, preact, 0.0).astype(BF16)

    far_keep, far_send = decode(ids, active, w_dec, groups[1:], pair, pair_rows, far_rows)
    sent = (far_keep + swap(far_send, "seq", 1).astype(F32)).astype(BF16)
    sent = [sent[i * rows : (i + 1) * rows] for i in range(size // 2 - 1)]
    near_active, sent = lax.optimization_barrier((active, sent))
    parts = [swap(piece, "seq", 2 * d + 2).astype(F32) for d, piece in enumerate(sent)]
    near_keep, near_send = decode(ids, near_active, w_dec, groups[:1], pair, 0, pair_rows)
    parts = [near_keep + swap(near_send, "seq", 1).astype(F32)] + parts
    predicted = tree_sum(parts) + b_dec
    reconstruction = predicted.astype(BF16)
    residual = (predicted - target.astype(F32)).astype(BF16)

    near_resid, even_resid, odd_resid = exchange(residual)
    back = pick(ids, none, near_resid, w_dec, 0, None)
    far_resid = even_resid + odd_resid
    back = pick(ids, back, far_resid, w_dec, pair_rows, None)
    slope = jnp.where(gate, sum_over(back, "tp"), 0.0)
    resid = near_resid + far_resid
    grad_dec = grad_rows(ids, active, resid, features)
    grad_enc = grad_rows(ids, slope.astype(BF16), near_tokens + far_tokens, features)
    grad_benc = bias_grad(ids, slope, features)
    groups, _ = lax.optimization_barrier((groups, back))
    mine = [lax.dynamic_slice_in_dim(g, (me % 2) * height, height, 1) for g in groups]
    other = [lax.dynamic_slice_in_dim(g, (1 - me % 2) * height, height, 1) for g in groups]
    others = swap(jnp.concatenate(other), "seq", 1)
    others = [others[i * rows : (i + 1) * rows] for i in range(size // 2)]
    grad_skip, grad_bdec = skip_grad([mine[0], others[0]] + mine[1:] + others[1:], resid)
    return reconstruction, grad_enc, grad_dec, grad_benc, grad_bdec, grad_skip


def solution(mesh):
    in_specs = (
        P("seq", "tp"),
        P("seq", "tp"),
        P(None, "seq", None),
        P("seq", "tp"),
        P("seq"),
        P("seq", "tp"),
        P("tp"),
        P("seq", "tp"),
    )
    out_specs = (P("seq", "tp"), P("seq", "tp"), P("seq", "tp"), P("seq"), P("tp"), P("seq", "tp"))
    return jax.shard_map(work, mesh=mesh, in_specs=in_specs, out_specs=out_specs, check_vma=False)
```
